32 devices in a mesh: rep: 4 (over y, x), fsdp: 8 (over z, core).
Axes of the slice: x: 2, y: 2, z: 4, core: 2. Of those that a mesh axis runs over, the one named last changes fastest.
Arguments:
- tokens: bfloat16 [6144, 4096], P(('rep', 'fsdp')), may hold values from -6 to 6
- cotangent: bfloat16 [6144, 256], P(('rep', 'fsdp')), may hold values from -6 to 6
- weight: float32 [4096, 256], P('fsdp'), may hold values from -0.09375 to 0.09375
- momentum: float32 [4, 4096, 256], P('rep', 'fsdp'), may hold values from -6 to 6
- column_order: int32 [64], replicated, may hold values from 0 to 63, each once
Outputs:
- input_grad: bfloat16 [6144, 4096], P(('rep', 'fsdp'))
- new_momentum: float32 [4, 4096, 256], P('rep', 'fsdp')
- update: float32 [4096, 256], P('fsdp')
- new_weight: float32 [4096, 256], P('fsdp')
The draws below stay inside these ranges and needn't reach their ends.
Inputs may be any that keep to these rules, and one draw needn't show every extreme that they name: `column_order`: each of the 64 frequency indices appears exactly once.
All inputs are finite; a program needn't handle non-finite values.
Results may differ from the reference program's by a relative error of at most 0.0049.
Values may be sent and summed in bfloat16 or wider, within the bound.
No kernel may reach another device: no remote copies, remote signals or barrier semaphores. Data moves between devices by JAX's collectives and lax.ppermute only.
A program may use at most 64 MiB of HBM per device.

```python
import math
import jax
import jax.numpy as jnp
from jax import lax

D = 4096
KW = 256
BLOCK = 64
SEL = 16
GROUP_TOK = 1536
ALL_TOK = 6144
N_REP = 4


def strengthened(drawn, own_key, source, target, shards_of, factor):
    owner, partner = [(jnp.arange(drawn.shape[dim]) // (drawn.shape[dim] // shards_of)).reshape([-1 if axis == dim else 1 for axis in range(drawn.ndim)]) for dim in (source, target)]
    chosen = jax.random.permutation(own_key, shards_of)[partner]
    strong = (owner == chosen) | (owner == (partner + shards_of // 2) % shards_of)
    return jnp.where(strong, factor * drawn, drawn)


def block_scale(rng, dims, shards, least, top_value):
    factor_of = 1.0
    for axis_at, parts in shards:
        heights = jax.random.uniform(jax.random.fold_in(jax.random.fold_in(rng, 6), axis_at), (parts,), jnp.float32, least / len(shards), top_value / len(shards))
        factor_of = factor_of * jnp.repeat(jnp.exp(heights), dims[axis_at] // parts).reshape((-1,) + (1,) * (len(dims) - 1 - axis_at))
    return factor_of


def centred(key, shape, deviation, bound, split=(), kind=jnp.bfloat16):
    entries = jax.random.normal(key, shape, jnp.float32) * deviation
    if len(split) > 0:
        entries = block_scale(key, shape, split, -0.22, 0.18) * entries
    return jnp.clip(entries, min=-bound, max=bound).astype(kind)


def noise_with(rng, extent, deviation, limit, cuts, heavy, dtype=jnp.bfloat16):
    result = deviation * jax.random.normal(rng, extent, jnp.float32)
    if cuts:
        result = result * block_scale(rng, extent, cuts, -0.22, 0.18)
    return jnp.clip(strengthened(result, jax.random.fold_in(rng, 3), *heavy), -limit, limit).astype(dtype)


def setup_inputs(seed: int = 0) -> dict:
    key_list = jax.random.split(jax.random.key(seed), 6)
    tokens = noise_with(key_list[0], (ALL_TOK, D), 1.0, 6.0, ((0, 32),), (0, 1, 32, 2.75))
    cotangent = centred(key_list[1], (ALL_TOK, KW), 1.0, 6.0, ((0, 32),))
    weight = centred(key_list[2], (D, KW), D ** -0.5, 0.09375, ((0, 8),), jnp.float32)
    momentum = centred(key_list[3], (N_REP, D, KW), 1.0, 6.0, ((0, 4), (1, 8)), jnp.float32)
    column_order = jax.random.permutation(key_list[4], BLOCK).astype(jnp.int32)
    return {"tokens": tokens, "cotangent": cotangent, "weight": weight, "momentum": momentum, "column_order": column_order}


MOMENTUM_DECAY = 0.9
LEARN_RATE = 0.05

def dct_table():
    index = jnp.arange(BLOCK).astype(jnp.float32)
    table = jnp.cos(math.pi * (2.0 * index[None, :] + 1.0) * index[:, None] / (2.0 * BLOCK)) * math.sqrt(2.0 / BLOCK)
    return jnp.where(index[:, None] == 0.0, table * math.sqrt(0.5), table)

def forward_blocks(field, table):
    rows, cols = field.shape
    blocks = field.reshape(rows // BLOCK, BLOCK, cols // BLOCK, BLOCK)
    out = jnp.einsum('kn,anbm,lm->akbl', table, blocks, table, precision=lax.Precision.HIGHEST)
    return out.reshape(rows, cols)

def inverse_blocks(field, table):
    rows, cols = field.shape
    blocks = field.reshape(rows // BLOCK, BLOCK, cols // BLOCK, BLOCK)
    out = jnp.einsum('kn,akbl,lm->anbm', table, blocks, table, precision=lax.Precision.HIGHEST)
    return out.reshape(rows, cols)

def reference(tokens, cotangent, weight, momentum, column_order):
    table = dct_table()
    weight_half = weight.astype(jnp.bfloat16)
    chosen = jnp.any(jnp.arange(BLOCK).astype(jnp.int32)[:, None] == column_order[None, :SEL], axis=1)
    col_mask = jnp.tile(chosen.astype(jnp.float32), KW // BLOCK)
    tok_groups = tokens.reshape(N_REP, GROUP_TOK, D)
    cot_groups = cotangent.reshape(N_REP, GROUP_TOK, KW)
    scale = float(GROUP_TOK) ** (-0.5)

    def per_replica(items):
        tok_part, cot_part, moment_old = items
        input_part = lax.dot_general(cot_part, weight_half, (((1,), (1,)), ((), ())), preferred_element_type=jnp.float32).astype(jnp.bfloat16)
        weight_grad = lax.dot_general(tok_part, cot_part, (((0,), (0,)), ((), ())), preferred_element_type=jnp.float32) * scale
        moment = MOMENTUM_DECAY * moment_old + weight_grad
        coeffs = forward_blocks(moment, table)
        sent = coeffs * col_mask[None, :]
        return (input_part, moment - inverse_blocks(sent, table), sent)
    input_grad, new_momentum, sent = lax.map(per_replica, (tok_groups, cot_groups, momentum))
    update = inverse_blocks(lax.optimization_barrier(jnp.sum(sent, axis=0)), table) / N_REP
    new_weight = weight - LEARN_RATE * update
    return (input_grad.reshape(ALL_TOK, D), new_momentum, update, new_weight)
```

```python
import functools
import math

import jax
import jax.numpy as jnp
import numpy as np
from jax import lax
from jax.experimental import pallas as pl
from jax.experimental.pallas import tpu as pltpu
from jax.sharding import PartitionSpec as P

BLOCK = 64
SEL = 16
LANES = 128
CORES = 2

MOMENTUM_DECAY = 0.9
LEARN_RATE = 0.05
HIGHEST = lax.Precision.HIGHEST


def dct_rows(width):
    index = np.arange(BLOCK, dtype=np.float64)
    table = np.cos(math.pi * (2.0 * index[None, :] + 1.0) * index[:, None] / (2.0 * BLOCK))
    table *= math.sqrt(2.0 / BLOCK)
    table[0] *= math.sqrt(0.5)
    return np.tile(table, (1, width // BLOCK)).astype(np.float32)


def vmem(count):
    return [pl.BlockSpec(memory_space=pltpu.VMEM)] * count


SMEM = pl.BlockSpec(memory_space=pltpu.SMEM)


def call(kernel, name, outs, in_specs, flops, nbytes, scratch=()):
    return pl.pallas_call(
        kernel,
        name=name,
        out_shape=outs,
        in_specs=in_specs,
        out_specs=vmem(len(outs)),
        scratch_shapes=scratch,
        cost_estimate=pl.CostEstimate(flops=flops, bytes_accessed=nbytes, transcendentals=0),
        compiler_params=pltpu.CompilerParams(vmem_limit_bytes=32 << 20),
    )


def dot(a, b, dims, precision=None):
    return lax.dot_general(
        a, b, (dims, ((), ())), precision=precision, preferred_element_type=jnp.float32
    )


def prepare_kernel(place, order, rows, weight, half, share, basis, chosen):
    part = share.shape[0]
    half[...] = weight[...].astype(jnp.bfloat16)
    start = pl.multiple_of(place[0] * part, part)
    share[...] = weight[pl.ds(start, part), :].astype(jnp.bfloat16)
    for s in range(SEL):
        chosen[pl.ds(s, 1), :] = rows[pl.ds(order[s], 1), :]
    lane_block = lax.broadcasted_iota(jnp.int32, chosen.shape, 1) // BLOCK
    for b in range(basis.shape[0] // SEL):
        basis[pl.ds(b * SEL, SEL), :] = jnp.where(lane_block == b, chosen[...], 0.0)


def partial_kernel(place, own_tok, their_tok, own_cot, their_cot, *outs):
    step = pl.program_id(0)
    total = dot(own_tok[...], own_cot[...], ((0,), (0,)))
    total += dot(their_tok[...], their_cot[...], ((0,), (0,)))
    for k, out in enumerate(outs):

        @pl.when(step == k)
        def _():
            out[...] = total.astype(out.dtype)


def combine_kernel(scale, own, basis, momentum, *refs):
    parts, (moment, packed) = refs[:-2], refs[-2:]
    total = own[...]
    for part in parts:
        total += part[...].astype(jnp.float32)
    value = MOMENTUM_DECAY * momentum[0] + scale * total
    coded = dot(basis[...], value, ((1,), (1,)), HIGHEST)
    packed[...] = coded.astype(packed.dtype)
    moment[0] = value - dot(coded, basis[...], ((0,), (0,)), HIGHEST)


def update_kernel(replicas, basis, weight, *refs):
    parts, (update, new_weight) = refs[:-2], refs[-2:]
    total = parts[0][...].astype(jnp.float32)
    for part in parts[1:]:
        total += part[...].astype(jnp.float32)
    value = dot(total, basis[...], ((0,), (0,)), HIGHEST) * (1.0 / replicas)
    update[...] = value
    new_weight[...] = weight[...] - LEARN_RATE * value


def input_kernel(chips, replicas, place, cot, *refs):
    pieces, out = refs[:-1], refs[-1]
    rep, chip, core = place[0], place[1], place[2]
    per_core = len(pieces) // CORES
    rows = pieces[0].shape[0]
    part = rows // replicas
    for side in range(CORES):
        whose = lax.rem(core + side, CORES)
        own, parts = pieces[side * per_core], pieces[side * per_core + 1 : (side + 1) * per_core]
        start = pl.multiple_of((CORES * chip + whose) * rows, rows)
        out[:, pl.ds(start, rows)] = dot(cot[...], own[...], ((1,), (1,))).astype(out.dtype)
        for e, piece in enumerate(parts):
            for d in range(1, chips):
                begin = (CORES * (chip ^ d) + whose) * rows + (rep ^ e) * part
                begin = pl.multiple_of(begin, part)
                block = piece[pl.ds((d - 1) * part, part), :]
                out[:, pl.ds(begin, part)] = dot(cot[...], block, ((1,), (1,))).astype(out.dtype)


def tuned(tokens, cotangent, weight, momentum, column_order):
    members, replicas = lax.axis_size("fsdp"), lax.axis_size("rep")
    chips = members // CORES
    count, width = tokens.shape
    rows, features = weight.shape
    packed_rows = features // BLOCK * SEL
    half_type = jnp.bfloat16
    rep, member = lax.axis_index("rep"), lax.axis_index("fsdp")
    chip, core = member // CORES, member % CORES
    place = jnp.stack([rep, chip, core]).astype(jnp.int32)

    def across(x, axis, mask):
        size = lax.axis_size(axis)
        return lax.ppermute(x, axis, [(i, i ^ mask) for i in range(size)])

    swap = lambda x: across(x, "fsdp", 1)
    shape = jax.ShapeDtypeStruct

    their_tokens, their_cot = swap(tokens), swap(cotangent)

    part = rows // replicas
    half, share, basis = call(
        prepare_kernel,
        "prepare",
        (
            shape((rows, features), half_type),
            shape((part, features), half_type),
            shape((packed_rows, features), jnp.float32),
        ),
        [SMEM, SMEM] + vmem(2),
        0,
        rows * features * 8,
        [pltpu.VMEM((SEL, features), jnp.float32)],
    )(place, column_order, dct_rows(features), weight)
    shares = jnp.concatenate([across(share, "fsdp", CORES * d) for d in range(1, chips)])
    theirs_half = swap(half)
    spread = [shares] + [across(shares, "rep", e) for e in range(1, replicas)]
    theirs = [swap(x) for x in spread]

    far = list(range(chips - 1, 0, -1)) + [0]
    where = jnp.stack([CORES * (chip ^ d) + core for d in far]).astype(jnp.int32)
    tok_spec = pl.BlockSpec((count, rows), lambda i, w: (0, w[i]))
    cot_spec = pl.BlockSpec((count, features), lambda i, w: (0, 0))
    out_spec = pl.BlockSpec((rows, features), lambda i, w: (0, 0))
    partials = pl.pallas_call(
        partial_kernel,
        name="partials",
        out_shape=[shape((rows, features), half_type if d else jnp.float32) for d in far],
        grid_spec=pltpu.PrefetchScalarGridSpec(
            num_scalar_prefetch=1,
            grid=(chips,),
            in_specs=[tok_spec, tok_spec, cot_spec, cot_spec],
            out_specs=[out_spec] * chips,
        ),
        cost_estimate=pl.CostEstimate(
            flops=2 * CORES * count * rows * chips * features,
            bytes_accessed=2 * CORES * count * rows * chips,
            transcendentals=0,
        ),
    )(where, tokens, their_tokens, cotangent, their_cot)
    arrived = [across(x, "fsdp", CORES * d) for d, x in zip(far[:-1], partials[:-1])]

    scale = float(count * members) ** (-0.5)
    new_momentum, packed = call(
        functools.partial(combine_kernel, scale),
        "combine",
        (shape(momentum.shape, jnp.float32), shape((packed_rows, rows), half_type)),
        vmem(3 + len(arrived)),
        12 * rows * features * packed_rows,
        rows * features * 16,
    )(partials[-1], basis, momentum, *arrived)

    coded = [packed] + [across(packed, "rep", e) for e in range(1, replicas)]
    update, new_weight = call(
        functools.partial(update_kernel, replicas),
        "update",
        (shape(weight.shape, jnp.float32),) * 2,
        vmem(2 + replicas),
        12 * rows * features * packed_rows,
        rows * features * 12,
    )(basis, weight, *coded)

    pieces = [half] + spread + [theirs_half] + theirs
    (input_grad,) = call(
        functools.partial(input_kernel, chips, replicas),
        "input_grad",
        (shape((count, width), half_type),),
        [SMEM] + vmem(1 + len(pieces)),
        2 * count * width * features,
        2 * (count + features) * width,
    )(place, cotangent, *pieces)
    return input_grad, new_momentum, update, new_weight


def general(tokens, cotangent, weight, momentum, column_order):
    members, replicas = lax.axis_size("fsdp"), lax.axis_size("rep")
    features = weight.shape[1]
    whole = lax.all_gather(weight.astype(jnp.bfloat16), "fsdp", axis=0, tiled=True)
    input_grad = dot(cotangent, whole, ((1,), (1,))).astype(jnp.bfloat16)
    grad = lax.psum_scatter(
        dot(tokens, cotangent, ((0,), (0,))), "fsdp", scatter_dimension=0, tiled=True
    )
    moment = MOMENTUM_DECAY * momentum[0] + grad * float(tokens.shape[0] * members) ** (-0.5)
    lane_block = jnp.arange(features) // BLOCK
    chosen = jnp.asarray(dct_rows(features))[column_order[:SEL]]
    basis = jnp.concatenate(
        [jnp.where(lane_block == b, chosen, 0.0) for b in range(features // BLOCK)]
    )
    coded = dot(moment, basis, ((1,), (1,)), HIGHEST)
    new_momentum = (moment - dot(coded, basis, ((1,), (0,)), HIGHEST))[None]
    summed = jnp.sum(lax.all_gather(coded, "rep", axis=0), axis=0)
    update = dot(summed, basis, ((1,), (0,)), HIGHEST) / replicas
    return input_grad, new_momentum, update, weight - LEARN_RATE * update


def on_device(tokens, cotangent, weight, momentum, column_order):
    members, replicas = lax.axis_size("fsdp"), lax.axis_size("rep")
    chips = members // CORES
    powers = all(n & (n - 1) == 0 for n in (chips, replicas))
    fits = powers and members % CORES == 0 and weight.shape[0] % (replicas * LANES) == 0
    body = tuned if fits else general
    return body(tokens, cotangent, weight, momentum, column_order)


def solution(mesh):
    in_specs = (
        P(("rep", "fsdp"), None),
        P(("rep", "fsdp"), None),
        P("fsdp", None),
        P("rep", "fsdp", None),
        P(),
    )
    out_specs = (P(("rep", "fsdp"), None), P("rep", "fsdp", None), P("fsdp", None), P("fsdp", None))
    return jax.shard_map(
        on_device, mesh=mesh, in_specs=in_specs, out_specs=out_specs, check_vma=False
    )
```

```python
import functools
import math

import jax
import jax.numpy as jnp
import numpy as np
from jax import lax
from jax.experimental import pallas as pl
from jax.experimental.pallas import tpu as pltpu
from jax.sharding import PartitionSpec as P


BLOCK = 64
SEL = 16
CORES = 2
LINE = 4

MOMENTUM_DECAY = 0.9
LEARN_RATE = 0.05
HIGHEST = lax.Precision.HIGHEST
BF16, F32 = jnp.bfloat16, jnp.float32


SMEM = pl.BlockSpec(memory_space=pltpu.SMEM)


def vmem(count):
    return [pl.BlockSpec(memory_space=pltpu.VMEM)] * count


def dct_rows(width):
    index = np.arange(BLOCK, dtype=np.float64)
    table = np.cos(math.pi * (2.0 * index[None, :] + 1.0) * index[:, None] / (2.0 * BLOCK))
    table *= math.sqrt(2.0 / BLOCK)
    table[0] *= math.sqrt(0.5)
    return np.tile(table, (1, width // BLOCK)).astype(np.float32)


def call(kernel, outs, in_specs, flops, nbytes, scratch=()):
    run = pl.pallas_call(
        kernel,
        out_shape=outs,
        in_specs=in_specs,
        out_specs=vmem(len(outs)),
        scratch_shapes=scratch,
        cost_estimate=pl.CostEstimate(flops=flops, bytes_accessed=nbytes, transcendentals=0),
        compiler_params=pltpu.CompilerParams(vmem_limit_bytes=32 << 20),
    )
    return run


def dot(a, b, dims, precision=None):
    return lax.dot_general(
        a, b, (dims, ((), ())), precision=precision, preferred_element_type=F32
    )


def position():
    member = lax.axis_index("fsdp")
    return lax.axis_index("rep"), member // CORES, lax.rem(member, CORES)


def wide(ref):
    return ref[...].astype(F32)


def start_kernel(order, rows, weight, cot, half, share, basis, coded_cot, table):
    for s in range(BLOCK):
        table[pl.ds(s, 1), :] = rows[pl.ds(order[s], 1), :]
    features = basis.shape[1]
    blocks = features // BLOCK
    rest = BLOCK - SEL
    for b in range(blocks):
        inside = lax.broadcasted_iota(jnp.int32, (BLOCK, features), 1) // BLOCK == b
        block = jnp.where(inside, table[...], 0.0)
        basis[pl.ds(b * SEL, SEL), :] = block[:SEL]
        basis[pl.ds(blocks * SEL + b * rest, rest), :] = block[SEL:]
    half[...] = weight[...].astype(BF16)
    part = share.shape[0]
    begin = pl.multiple_of(lax.axis_index("rep") * part, part)
    share[...] = weight[pl.ds(begin, part), :].astype(BF16)
    coded_cot[...] = dot(basis[...], wide(cot), ((1,), (1,)), HIGHEST).astype(BF16)


def partial_kernel(mine, theirs, own_tok, their_tok, *outs):
    codes, (turn, near, keep, own_code, own_rest) = outs[:-5], outs[-5:]
    _, chip, core = position()
    sent, columns = own_code.shape

    def total(mask):
        dest = chip ^ mask
        at = pl.ds(pl.multiple_of((CORES * dest + core) * columns, columns), columns)
        value = dot(mine[...], own_tok[:, at], ((1,), (0,)))
        return value + dot(theirs[...], their_tok[:, at], ((1,), (0,)))

    for mask, out in ((2, turn), (1, near), (3, keep)):
        value = total(mask)
        codes[mask - 1][...] = value[:sent].astype(BF16)
        out[...] = value[sent:].astype(out.dtype)
    value = total(0)
    own_code[...] = value[:sent]
    own_rest[...] = value[sent:]


def middle():
    _, chip, _ = position()
    return jnp.logical_and(chip > 0, chip < LINE - 1)


def old_kernel(basis, momentum, kept, coded):
    sent = basis[: coded.shape[0], :]
    old = MOMENTUM_DECAY * momentum[0]
    code = dot(sent, old, ((1,), (1,)), HIGHEST)
    coded[...] = code
    kept[...] = old - dot(code, sent, ((0,), (0,)), HIGHEST)


def join_kernel(*refs):
    part = refs[0].shape[0]
    for k, ref in enumerate(refs[:-1]):
        refs[-1][pl.ds(k * part, part), :] = ref[...]


def relay_kernel(keep, turned, out):
    passed = jnp.where(middle(), wide(turned), 0.0)
    out[...] = (keep[...] + passed).astype(out.dtype)


def code_kernel(scale, coded, own, *refs):
    total = own[...]
    for part in refs[:-1]:
        total += wide(part)
    refs[-1][...] = (coded[...] + scale * total).astype(BF16)


def moment_kernel(scale, basis, kept, own, near, turned, late, out):
    total = own[...] + wide(near) + wide(late)
    total += jnp.where(middle(), 0.0, wide(turned))
    rest = basis[basis.shape[0] - own.shape[0] :, :]
    grad = dot(total.astype(BF16), rest.astype(BF16), ((0,), (0,)))
    out[0] = kept[...] + scale * grad


def update_kernel(replicas, basis, weight, *refs):
    parts, (update, new_weight) = refs[:-2], refs[-2:]
    total = wide(parts[0])
    for part in parts[1:]:
        total += wide(part)
    sent = basis[: total.shape[0], :]
    value = dot(total, sent, ((0,), (0,)), HIGHEST) * (1.0 / replicas)
    update[...] = value
    new_weight[...] = weight[...] - LEARN_RATE * value


def input_kernel(chips, cot, *refs):
    pieces, out = refs[:-1], refs[-1]
    rep, chip, core = position()
    per_core = len(pieces) // CORES
    rows = pieces[0].shape[0]
    part = rows // (per_core - 1)
    for side in range(CORES):
        whose = lax.rem(core + side, CORES)
        own, parts = pieces[side * per_core], pieces[side * per_core + 1 : (side + 1) * per_core]
        begin = pl.multiple_of((CORES * chip + whose) * rows, rows)
        out[:, pl.ds(begin, rows)] = dot(cot[...], own[...], ((1,), (1,))).astype(out.dtype)
        for e, piece in enumerate(parts):
            value = dot(cot[...], piece[...], ((1,), (1,))).astype(out.dtype)
            for d in range(1, chips):
                begin = (CORES * (chip ^ d) + whose) * rows + (rep ^ e) * part
                at = pl.ds(pl.multiple_of(begin, part), part)
                out[:, at] = value[:, (d - 1) * part : d * part]


def tuned(tokens, cotangent, weight, momentum, column_order):
    members, replicas = lax.axis_size("fsdp"), lax.axis_size("rep")
    chips = members // CORES
    count, width = tokens.shape
    rows, features = weight.shape
    sent = features // BLOCK * SEL
    part = rows // replicas
    masks = range(1, chips)
    shape = jax.ShapeDtypeStruct

    def permute(x, axis, target):
        pairs = [(i, target(i)) for i in range(lax.axis_size(axis))]
        return lax.ppermute(x, axis, pairs)

    def swap(x):
        return permute(x, "fsdp", lambda i: i ^ 1)

    def chip_hop(x, target):
        return permute(x, "fsdp", lambda i: CORES * target(i // CORES) + i % CORES)

    def over_chips(x, mask):
        return chip_hop(x, lambda z: z ^ mask)

    def over_rep(x):
        return [permute(x, "rep", lambda i, e=e: i ^ e) for e in range(1, replicas)]

    their_tokens = swap(tokens)
    half, share, basis, mine = call(
        start_kernel,
        (
            shape((rows, features), BF16),
            shape((part, features), BF16),
            shape((features, features), F32),
            shape((features, count), BF16),
        ),
        [SMEM] + [pl.BlockSpec()] * 3,
        12 * features * features * count,
        32 * count * width,
        [pltpu.VMEM((BLOCK, features), F32)],
    )(column_order, dct_rows(features), weight, cotangent)
    theirs = swap(mine)
    shares = [over_chips(share, d) for d in masks]

    code, rest = shape((sent, rows), BF16), shape((features - sent, rows), BF16)
    *codes, turn, near, keep, own_code, own_rest = call(
        partial_kernel,
        (code,) * len(masks) + (rest, rest, shape(rest.shape, F32), shape(code.shape, F32), shape(rest.shape, F32)),
        vmem(4),
        2 * CORES * count * rows * chips * features,
        CORES * count * rows * chips * 2,
    )(mine, theirs, tokens, their_tokens)

    way = (1, 3, 0, 2)
    turned = chip_hop(turn, lambda z: way[z])
    codes = [over_chips(x, d) for d, x in zip(masks, codes)]
    near = over_chips(near, 1)
    (late,) = call(relay_kernel, (rest,), vmem(2), 0, rest.size * 8)(keep, turned)
    late = over_chips(late, LINE - 1)

    kept, coded = call(
        old_kernel,
        (shape((rows, features), F32), shape((sent, rows), F32)),
        vmem(2),
        24 * rows * features * sent,
        rows * features * 8,
    )(basis, momentum)
    scale = float(count * members) ** (-0.5)
    (packed,) = call(
        functools.partial(code_kernel, scale), (code,), vmem(2 + len(codes)), 0, sent * rows * 18
    )(coded, own_code, *codes)
    update, new_weight = call(
        functools.partial(update_kernel, replicas),
        (shape(weight.shape, F32),) * 2,
        vmem(2 + replicas),
        12 * rows * features * sent,
        rows * features * 12,
    )(basis, weight, packed, *over_rep(packed))
    (new_momentum,) = call(
        functools.partial(moment_kernel, scale),
        (shape(momentum.shape, F32),),
        vmem(6),
        2 * rows * features * features,
        rows * features * 16,
    )(basis, kept, own_rest, near, turned, late)

    (joined,) = call(
        join_kernel,
        (shape((part * len(shares), features), BF16),),
        vmem(len(shares)),
        0,
        part * len(shares) * features * 4,
    )(*shares)
    pieces = [half, joined] + over_rep(joined)
    pieces += [swap(x) for x in pieces]
    (input_grad,) = call(
        functools.partial(input_kernel, chips),
        (shape((count, width), BF16),),
        vmem(1 + len(pieces)),
        2 * count * width * features,
        2 * (count + features) * width,
    )(cotangent, *pieces)
    return input_grad, new_momentum, update, new_weight


def general(tokens, cotangent, weight, momentum, column_order):
    members, replicas = lax.axis_size("fsdp"), lax.axis_size("rep")
    features = weight.shape[1]
    whole = lax.all_gather(weight.astype(BF16), "fsdp", axis=0, tiled=True)
    input_grad = dot(cotangent, whole, ((1,), (1,))).astype(BF16)
    grad = lax.psum_scatter(
        dot(tokens, cotangent, ((0,), (0,))), "fsdp", scatter_dimension=0, tiled=True
    )
    moment = MOMENTUM_DECAY * momentum[0] + grad * float(tokens.shape[0] * members) ** (-0.5)
    lane_block = jnp.arange(features) // BLOCK
    chosen = jnp.asarray(dct_rows(features))[column_order[:SEL]]
    basis = jnp.concatenate(
        [jnp.where(lane_block == b, chosen, 0.0) for b in range(features // BLOCK)]
    )
    coded = dot(moment, basis, ((1,), (1,)), HIGHEST)
    new_momentum = (moment - dot(coded, basis, ((1,), (0,)), HIGHEST))[None]
    summed = jnp.sum(lax.all_gather(coded, "rep", axis=0), axis=0)
    update = dot(summed, basis, ((1,), (0,)), HIGHEST) / replicas
    return input_grad, new_momentum, update, weight - LEARN_RATE * update


def solution(mesh):
    in_specs = (
        P(("rep", "fsdp"), None),
        P(("rep", "fsdp"), None),
        P("fsdp", None),
        P("rep", "fsdp", None),
        P(),
    )
    out_specs = (P(("rep", "fsdp"), None), P("rep", "fsdp", None), P("fsdp", None), P("fsdp", None))
    members, replicas = mesh.shape["fsdp"], mesh.shape["rep"]
    line = members == LINE * CORES and replicas == LINE

    def on_device(*args):
        if not line:
            return general(*args)
        return tuned(*args)

    return jax.shard_map(
        on_device, mesh=mesh, in_specs=in_specs, out_specs=out_specs, check_vma=False
    )
```

```python
import functools
import math

import jax
import jax.numpy as jnp
import numpy as np
from jax import lax
from jax.experimental import pallas as pl
from jax.experimental.pallas import tpu as pltpu
from jax.sharding import PartitionSpec as P


BLOCK = 64
SEL = 16
CORES = 2
CHIPS = 4

MOMENTUM_DECAY = 0.9
LEARN_RATE = 0.05
HIGHEST = lax.Precision.HIGHEST
BF16, F32 = jnp.bfloat16, jnp.float32


HBM = pl.BlockSpec(memory_space=pltpu.HBM)


def vmem(count):
    return [pl.BlockSpec(memory_space=pltpu.VMEM)] * count


def dct_rows(width):
    index = np.arange(BLOCK, dtype=np.float64)
    table = np.cos(math.pi * (2.0 * index[None, :] + 1.0) * index[:, None] / (2.0 * BLOCK))
    table *= math.sqrt(2.0 / BLOCK)
    table[0] *= math.sqrt(0.5)
    return np.tile(table, (1, width // BLOCK)).astype(np.float32)


def call(kernel, outs, in_specs, flops, nbytes, scratch=(), limit=32 << 20):
    run = pl.pallas_call(
        kernel,
        out_shape=outs,
        in_specs=in_specs,
        out_specs=vmem(len(outs)),
        scratch_shapes=scratch,
        cost_estimate=pl.CostEstimate(flops=flops, bytes_accessed=nbytes, transcendentals=0),
        compiler_params=pltpu.CompilerParams(vmem_limit_bytes=limit),
    )
    return run


def dot(a, b, dims, precision=None):
    return lax.dot_general(
        a, b, (dims, ((), ())), precision=precision, preferred_element_type=F32
    )


def halves(x):
    high = x.astype(BF16)
    return high, (x - high.astype(F32)).astype(BF16)


def outer(a, b):
    (a_high, a_low), (b_high, b_low) = halves(a), halves(b)
    left = jnp.concatenate([a_high, a_low, a_high])
    return dot(left, jnp.concatenate([b_high, b_high, b_low]), ((0,), (0,)))


def position():
    member = lax.axis_index("fsdp")
    return lax.axis_index("rep"), member // CORES, lax.rem(member, CORES)


def in_hbm(x):
    return pltpu.with_memory_space_constraint(x, pltpu.HBM)


def wide(ref):
    return ref[...].astype(F32)


def start_kernel(order, rows, weight, cot, tokens, *refs):
    half, share, basis, coded_cot, own = refs[:5]
    held_order, held_rows, held_weight, held_cot, table, sems = refs[5:]
    rep, _, core = position()
    columns = weight.shape[0]
    moves = [(weight, held_weight), (order, held_order), (rows, held_rows), (cot, held_cot)]
    for k in range(own.shape[1] // columns):
        at = pl.ds(pl.multiple_of((CORES * k + core) * columns, columns), columns)
        moves.append((tokens.at[:, at], own.at[:, pl.ds(k * columns, columns)]))
    copies = [pltpu.make_async_copy(a, b, sems.at[k]) for k, (a, b) in enumerate(moves)]
    for copy in copies:
        copy.start()
    copies[0].wait()
    half[...] = held_weight[...].astype(BF16)
    part = share.shape[0]
    begin = pl.multiple_of(rep * part, part)
    share[...] = held_weight[pl.ds(begin, part), :].astype(BF16)
    copies[1].wait()
    copies[2].wait()
    for s in range(BLOCK):
        table[pl.ds(s, 1), :] = held_rows[pl.ds(held_order[s], 1), :]
    features = basis.shape[1]
    blocks = features // BLOCK
    rest = BLOCK - SEL
    for b in range(blocks):
        inside = lax.broadcasted_iota(jnp.int32, (BLOCK, features), 1) // BLOCK == b
        block = jnp.where(inside, table[...], 0.0)
        basis[pl.ds(b * SEL, SEL), :] = block[:SEL]
        basis[pl.ds(blocks * SEL + b * rest, rest), :] = block[SEL:]
    copies[3].wait()
    high, low = halves(basis[...])
    value = dot(high, held_cot[...], ((1,), (1,))) + dot(low, held_cot[...], ((1,), (1,)))
    coded_cot[...] = value.astype(BF16)
    for copy in copies[4:]:
        copy.wait()


def partial_kernel(mine, theirs, own_tok, their_tok, *outs):
    code, keep_code, own_code, far, near, keep, own_rest = outs
    _, chip, core = position()
    sent, columns = own_code.shape

    def total(mask):
        dest = chip ^ mask
        own_at = pl.ds(pl.multiple_of(dest * columns, columns), columns)
        at = pl.ds(pl.multiple_of((CORES * dest + core) * columns, columns), columns)
        value = dot(mine[...], own_tok[:, own_at], ((1,), (0,)))
        return value + dot(theirs[...], their_tok[:, at], ((1,), (0,)))

    first, last = code.at[pl.ds(0, sent), :], code.at[pl.ds(sent, sent), :]
    for mask, head, rest in (
        (1, first, near),
        (3, last, far),
        (2, keep_code, keep),
        (0, own_code, own_rest),
    ):
        value = total(mask)
        head[...] = value[:sent].astype(head.dtype)
        rest[...] = value[sent:].astype(rest.dtype)


def old_kernel(basis, momentum, kept, coded):
    sent = basis[: coded.shape[0], :]
    old = MOMENTUM_DECAY * momentum[0]
    (sent_high, sent_low), (high, low) = halves(sent), halves(old)
    code = dot(sent_high, high, ((1,), (1,))) + dot(sent_high, low, ((1,), (1,)))
    code += dot(sent_low, high, ((1,), (1,)))
    coded[...] = code
    kept[...] = old - outer(code, sent)


def join_kernel(*refs):
    at = 0
    for ref in refs[:-1]:
        refs[-1][pl.ds(at, ref.shape[0]), :] = ref[...]
        at += ref.shape[0]


def relay_kernel(keep, arrived, out):
    out[...] = (keep[...] + wide(arrived)).astype(out.dtype)


def code_kernel(keep, arrived, out):
    out[...] = (keep[...] + arrived[keep.shape[0] :, :].astype(F32)).astype(out.dtype)


def pack_kernel(scale, coded, own, arrived, late, out):
    total = own[...] + arrived[: own.shape[0], :].astype(F32) + wide(late)
    out[...] = (coded[...] + scale * total).astype(out.dtype)


def add_kernel(left, right, out):
    out[...] = (wide(left) + wide(right)).astype(out.dtype)


def moment_kernel(scale, basis, kept, own, near, late, out):
    total = own[...] + wide(near) + wide(late)
    rest = basis[basis.shape[0] - own.shape[0] :, :]
    grad = dot(total.astype(BF16), rest.astype(BF16), ((0,), (0,)))
    out[0] = kept[...] + scale * grad


def update_kernel(replicas, basis, weight, left, right, update, new_weight):
    total = wide(left) + wide(right)
    sent = basis[: total.shape[0], :]
    value = outer(total, sent) * (1.0 / replicas)
    update[...] = value
    new_weight[...] = weight[...] - LEARN_RATE * value


def input_kernel(chips, replicas, cot, *refs):
    pieces, out = refs[:-1], refs[-1]
    rep, chip, core = position()
    rows = pieces[0].shape[0]
    part = rows // replicas
    group = part * (chips - 1)
    for side in range(CORES):
        whose = lax.rem(core + side, CORES)
        own, others = pieces[2 * side : 2 * side + 2]
        begin = pl.multiple_of((CORES * chip + whose) * rows, rows)
        out[:, pl.ds(begin, rows)] = dot(cot[...], own[...], ((1,), (1,))).astype(out.dtype)
        for e in range(replicas):
            piece = others[e * group : (e + 1) * group, :]
            value = dot(cot[...], piece, ((1,), (1,))).astype(out.dtype)
            for d in range(1, chips):
                begin = (CORES * (chip ^ d) + whose) * rows + (rep ^ e) * part
                at = pl.ds(pl.multiple_of(begin, part), part)
                out[:, at] = value[:, (d - 1) * part : d * part]


def tuned(tokens, cotangent, weight, momentum, column_order):
    members, replicas = lax.axis_size("fsdp"), lax.axis_size("rep")
    chips = members // CORES
    count, width = tokens.shape
    rows, features = weight.shape
    sent = features // BLOCK * SEL
    part = rows // replicas
    shape = jax.ShapeDtypeStruct

    def permute(x, axis, target):
        pairs = [(i, target(i)) for i in range(lax.axis_size(axis))]
        return lax.ppermute(x, axis, pairs)

    def swap(x):
        return permute(x, "fsdp", lambda i: i ^ 1)

    def over_chips(x, mask):
        return permute(x, "fsdp", lambda i: i ^ (CORES * mask))

    def over_rep(x, mask):
        return permute(x, "rep", lambda i: i ^ mask)

    def simple(kernel, out, *args):
        (value,) = call(kernel, (out,), vmem(len(args)), 0, 8 * out.size)(*args)
        return value

    def join(*args):
        size = sum(x.shape[0] for x in args)
        return simple(join_kernel, shape((size, args[0].shape[1]), args[0].dtype), *args)

    their_tokens = swap(tokens)
    half, share, basis, mine, own_tokens = call(
        start_kernel,
        (
            shape((rows, features), BF16),
            shape((part, features), BF16),
            shape((features, features), F32),
            shape((features, count), BF16),
            shape((count, chips * rows), BF16),
        ),
        [HBM] * 5,
        12 * features * features * count,
        2 * count * width,
        [
            pltpu.SMEM((BLOCK,), jnp.int32),
            pltpu.VMEM((BLOCK, features), F32),
            pltpu.VMEM((rows, features), F32),
            pltpu.VMEM((count, features), BF16),
            pltpu.VMEM((BLOCK, features), F32),
            pltpu.SemaphoreType.DMA((4 + chips,)),
        ],
    )(*map(in_hbm, (column_order, jnp.asarray(dct_rows(features)), weight, cotangent, tokens)))
    theirs = swap(mine)
    shares = [over_chips(share, d) for d in range(1, chips)]

    code, rest = shape((sent, rows), BF16), shape((features - sent, rows), BF16)
    code_f32, rest_f32 = shape(code.shape, F32), shape(rest.shape, F32)
    codes, keep_code, own_code, far, near, keep, own_rest = call(
        partial_kernel,
        (shape((2 * sent, rows), BF16), code_f32, code_f32, rest, rest, rest_f32, rest_f32),
        vmem(4),
        2 * CORES * count * rows * chips * features,
        CORES * count * rows * chips * 2,
    )(mine, theirs, own_tokens, their_tokens)

    codes = over_chips(codes, 1)
    far = over_chips(far, 1)
    near = over_chips(near, 1)
    late_code = over_chips(simple(code_kernel, code, keep_code, codes), 2)
    late = over_chips(simple(relay_kernel, rest, keep, far), 2)

    kept, coded = call(
        old_kernel,
        (shape((rows, features), F32), shape((sent, rows), F32)),
        vmem(2),
        24 * rows * features * sent,
        rows * features * 8,
    )(basis, momentum)
    scale = float(count * members) ** (-0.5)
    packed = simple(functools.partial(pack_kernel, scale), code, coded, own_code, codes, late_code)
    paired = simple(add_kernel, code, packed, over_rep(packed, 1))
    update, new_weight = call(
        functools.partial(update_kernel, replicas),
        (shape(weight.shape, F32),) * 2,
        vmem(4),
        12 * rows * features * sent,
        rows * features * 12,
    )(basis, weight, paired, over_rep(paired, 2))
    (new_momentum,) = call(
        functools.partial(moment_kernel, scale),
        (shape(momentum.shape, F32),),
        vmem(5),
        2 * rows * features * features,
        rows * features * 16,
    )(basis, kept, own_rest, near, late)

    joined = join(*shares)
    spread = [over_rep(joined, e) for e in range(1, replicas)]
    gathered = join(joined, *spread)
    pieces = [half, gathered, swap(half), swap(gathered)]
    (input_grad,) = call(
        functools.partial(input_kernel, chips, replicas),
        (shape((count, width), BF16),),
        vmem(1 + len(pieces)),
        2 * count * width * features,
        2 * (count + features) * width,
    )(cotangent, *pieces)
    return input_grad, new_momentum, update, new_weight


def general(tokens, cotangent, weight, momentum, column_order):
    members, replicas = lax.axis_size("fsdp"), lax.axis_size("rep")
    features = weight.shape[1]
    whole = lax.all_gather(weight.astype(BF16), "fsdp", axis=0, tiled=True)
    input_grad = dot(cotangent, whole, ((1,), (1,))).astype(BF16)
    grad = lax.psum_scatter(
        dot(tokens, cotangent, ((0,), (0,))), "fsdp", scatter_dimension=0, tiled=True
    )
    moment = MOMENTUM_DECAY * momentum[0] + grad * float(tokens.shape[0] * members) ** (-0.5)
    lane_block = jnp.arange(features) // BLOCK
    chosen = jnp.asarray(dct_rows(features))[column_order[:SEL]]
    basis = jnp.concatenate(
        [jnp.where(lane_block == b, chosen, 0.0) for b in range(features // BLOCK)]
    )
    coded = dot(moment, basis, ((1,), (1,)), HIGHEST)
    new_momentum = (moment - dot(coded, basis, ((1,), (0,)), HIGHEST))[None]
    summed = jnp.sum(lax.all_gather(coded, "rep", axis=0), axis=0)
    update = dot(summed, basis, ((1,), (0,)), HIGHEST) / replicas
    return input_grad, new_momentum, update, weight - LEARN_RATE * update


def solution(mesh):
    in_specs = (
        P(("rep", "fsdp"), None),
        P(("rep", "fsdp"), None),
        P("fsdp", None),
        P("rep", "fsdp", None),
        P(),
    )
    out_specs = (P(("rep", "fsdp"), None), P("rep", "fsdp", None), P("fsdp", None), P("fsdp", None))
    members, replicas = mesh.shape["fsdp"], mesh.shape["rep"]
    line = members == CHIPS * CORES and replicas == CHIPS

    def on_device(*args):
        if not line:
            return general(*args)
        return tuned(*args)

    return jax.shard_map(
        on_device, mesh=mesh, in_specs=in_specs, out_specs=out_specs, check_vma=False
    )
```

```python
import functools
import math

import jax
import jax.numpy as jnp
import numpy as np
from jax import lax
from jax.experimental import pallas as pl
from jax.experimental.pallas import tpu as pltpu
from jax.sharding import PartitionSpec as P


BLOCK = 64
SEL = 16
CORES = 2
CHIPS = 4
ARRIVAL = (1, 2, 3)

MOMENTUM_DECAY = 0.9
LEARN_RATE = 0.05
HIGHEST = lax.Precision.HIGHEST
BF16, F32 = jnp.bfloat16, jnp.float32


HBM = pl.BlockSpec(memory_space=pltpu.HBM)


def vmem(count):
    return [pl.BlockSpec(memory_space=pltpu.VMEM)] * count


def dct_rows(width):
    index = np.arange(BLOCK, dtype=np.float64)
    table = np.cos(math.pi * (2.0 * index[None, :] + 1.0) * index[:, None] / (2.0 * BLOCK))
    table *= math.sqrt(2.0 / BLOCK)
    table[0] *= math.sqrt(0.5)
    return np.tile(table, (1, width // BLOCK)).astype(np.float32)


def call(kernel, outs, in_specs, flops, nbytes, scratch=(), out_spec=None, aliases=None):
    run = pl.pallas_call(
        kernel,
        out_shape=outs,
        in_specs=in_specs,
        out_specs=[out_spec or pl.BlockSpec(memory_space=pltpu.VMEM)] * len(outs),
        input_output_aliases=aliases or {},
        scratch_shapes=scratch,
        cost_estimate=pl.CostEstimate(flops=flops, bytes_accessed=nbytes, transcendentals=0),
        compiler_params=pltpu.CompilerParams(vmem_limit_bytes=32 << 20),
    )
    return run


def dot(a, b, dims, precision=None):
    return lax.dot_general(
        a, b, (dims, ((), ())), precision=precision, preferred_element_type=F32
    )


def halves(x):
    high = x.astype(BF16)
    return high, (x - high.astype(F32)).astype(BF16)


def outer(a, b):
    (a_high, a_low), (b_high, b_low) = halves(a), halves(b)
    left = jnp.concatenate([a_high, a_low, a_high])
    return dot(left, jnp.concatenate([b_high, b_high, b_low]), ((0,), (0,)))


def position():
    member = lax.axis_index("fsdp")
    return lax.axis_index("rep"), member // CORES, lax.rem(member, CORES)


def in_hbm(x):
    return pltpu.with_memory_space_constraint(x, pltpu.HBM)


def wide(ref):
    return ref[...].astype(F32)


def start_kernel(order, rows, weight, cot, tokens, *refs):
    half, share, basis, coded_cot, own = refs[:5]
    held_order, held_rows, held_weight, held_cot, table, sems = refs[5:]
    rep, _, core = position()
    columns = weight.shape[0]
    moves = [(weight, held_weight), (order, held_order), (rows, held_rows), (cot, held_cot)]
    for k in range(own.shape[1] // columns):
        at = pl.ds(pl.multiple_of((CORES * k + core) * columns, columns), columns)
        moves.append((tokens.at[:, at], own.at[:, pl.ds(k * columns, columns)]))
    copies = [pltpu.make_async_copy(a, b, sems.at[k]) for k, (a, b) in enumerate(moves)]
    for copy in copies:
        copy.start()
    copies[0].wait()
    half[...] = held_weight[...].astype(BF16)
    part = share.shape[0]
    begin = pl.multiple_of(rep * part, part)
    share[...] = held_weight[pl.ds(begin, part), :].astype(BF16)
    copies[1].wait()
    copies[2].wait()
    for s in range(BLOCK):
        table[pl.ds(s, 1), :] = held_rows[pl.ds(held_order[s], 1), :]
    features = basis.shape[1]
    blocks = features // BLOCK
    rest = BLOCK - SEL
    for b in range(blocks):
        inside = lax.broadcasted_iota(jnp.int32, (BLOCK, features), 1) // BLOCK == b
        block = jnp.where(inside, table[...], 0.0)
        basis[pl.ds(b * SEL, SEL), :] = block[:SEL]
        basis[pl.ds(blocks * SEL + b * rest, rest), :] = block[SEL:]
    copies[3].wait()
    high, low = halves(basis[...])
    value = dot(high, held_cot[...], ((1,), (1,))) + dot(low, held_cot[...], ((1,), (1,)))
    coded_cot[...] = value.astype(BF16)
    for copy in copies[4:]:
        copy.wait()


def partial_kernel(mine, theirs, own_tok, their_tok, *outs):
    code, keep_code, own_code, far, near, keep, own_rest = outs
    _, chip, core = position()
    sent, columns = own_code.shape

    def total(mask):
        dest = chip ^ mask
        own_at = pl.ds(pl.multiple_of(dest * columns, columns), columns)
        at = pl.ds(pl.multiple_of((CORES * dest + core) * columns, columns), columns)
        value = dot(mine[...], own_tok[:, own_at], ((1,), (0,)))
        return value + dot(theirs[...], their_tok[:, at], ((1,), (0,)))

    first, last = code.at[pl.ds(0, sent), :], code.at[pl.ds(sent, sent), :]
    for mask, head, rest in (
        (1, first, near),
        (3, last, far),
        (2, keep_code, keep),
        (0, own_code, own_rest),
    ):
        value = total(mask)
        head[...] = value[:sent].astype(head.dtype)
        rest[...] = value[sent:].astype(rest.dtype)


def old_kernel(basis, momentum, kept, coded):
    sent = basis[: coded.shape[0], :]
    old = MOMENTUM_DECAY * momentum[0]
    (sent_high, sent_low), (high, low) = halves(sent), halves(old)
    code = dot(sent_high, high, ((1,), (1,))) + dot(sent_high, low, ((1,), (1,)))
    code += dot(sent_low, high, ((1,), (1,)))
    coded[...] = code
    kept[...] = old - outer(code, sent)


def join_kernel(*refs):
    at = 0
    for ref in refs[:-1]:
        refs[-1][pl.ds(at, ref.shape[0]), :] = ref[...]
        at += ref.shape[0]


def relay_kernel(keep, arrived, out):
    out[...] = (keep[...] + wide(arrived)).astype(out.dtype)


def code_kernel(keep, arrived, out):
    out[...] = (keep[...] + arrived[keep.shape[0] :, :].astype(F32)).astype(out.dtype)


def pack_kernel(scale, coded, own, arrived, late, out):
    total = own[...] + arrived[: own.shape[0], :].astype(F32) + wide(late)
    out[...] = (coded[...] + scale * total).astype(out.dtype)


def add_kernel(left, right, out):
    out[...] = (wide(left) + wide(right)).astype(out.dtype)


def final_kernel(scale, replicas, basis, kept, own, near, late, weight, left, right, *refs):
    (moment, update, new_weight), (stage, sems) = refs[:3], refs[3:]
    total = own[...] + wide(near) + wide(late)
    rest = basis[basis.shape[0] - own.shape[0] :, :]
    grad = dot(total.astype(BF16), rest.astype(BF16), ((0,), (0,)))
    stage[0] = kept[...] + scale * grad
    copies = [
        pltpu.make_async_copy(stage.at[0], moment.at[0], sems.at[0]),
        pltpu.make_async_copy(stage.at[1], update, sems.at[1]),
        pltpu.make_async_copy(stage.at[2], new_weight, sems.at[2]),
    ]
    copies[0].start()
    code = wide(left) + wide(right)
    value = outer(code, basis[: code.shape[0], :]) * (1.0 / replicas)
    stage[1] = value
    copies[1].start()
    stage[2] = weight[...] - LEARN_RATE * value
    copies[2].start()
    for copy in copies:
        copy.wait()


def send_blocks(cot, piece, blocks, stage, out, sems, done):
    start = sum(size for _, size in done)
    stage[:, pl.ds(start, piece.shape[0])] = dot(cot[...], piece, ((1,), (1,))).astype(stage.dtype)
    for begin, size in blocks:
        to = out.at[:, pl.ds(pl.multiple_of(begin, size), size)]
        copy = pltpu.make_async_copy(stage.at[:, pl.ds(start, size)], to, sems.at[len(done)])
        copy.start()
        done.append((copy, size))
        start += size


def places(rows, replicas, side, e):
    rep, chip, core = position()
    part = rows // replicas
    whose = lax.rem(core + side, CORES)
    return [((CORES * (chip ^ d) + whose) * rows + (rep ^ e) * part, part) for d in ARRIVAL]


def early_kernel(replicas, rows, cot, mine, theirs, out, stage, sems):
    _, chip, core = position()
    done = []
    for side, piece in enumerate((mine, theirs)):
        begin = (CORES * chip + lax.rem(core + side, CORES)) * rows
        blocks = places(rows, replicas, side, 0)
        send_blocks(cot, piece[:rows, :], [(begin, rows)], stage, out, sems, done)
        send_blocks(cot, piece[rows:, :], blocks, stage, out, sems, done)
    for copy, _ in done:
        copy.wait()


def later_kernel(replicas, rows, _, cot, mine, theirs, out, stage, sems):
    done = []
    group = rows // replicas * len(ARRIVAL)
    for side, piece in enumerate((mine, theirs)):
        for e in range(1, replicas):
            block = piece[(e - 1) * group : e * group, :]
            send_blocks(cot, block, places(rows, replicas, side, e), stage, out, sems, done)
    for copy, _ in done:
        copy.wait()


def tuned(tokens, cotangent, weight, momentum, column_order):
    members, replicas = lax.axis_size("fsdp"), lax.axis_size("rep")
    chips = members // CORES
    count, width = tokens.shape
    rows, features = weight.shape
    sent = features // BLOCK * SEL
    part = rows // replicas
    shape = jax.ShapeDtypeStruct

    def permute(x, axis, target):
        pairs = [(i, target(i)) for i in range(lax.axis_size(axis))]
        return lax.ppermute(x, axis, pairs)

    def swap(x):
        return permute(x, "fsdp", lambda i: i ^ 1)

    def over_chips(x, mask):
        return permute(x, "fsdp", lambda i: i ^ (CORES * mask))

    def over_rep(x, mask):
        return permute(x, "rep", lambda i: i ^ mask)

    def simple(kernel, out, *args):
        (value,) = call(kernel, (out,), vmem(len(args)), 0, 8 * out.size)(*args)
        return value

    def join(*args):
        size = sum(x.shape[0] for x in args)
        return simple(join_kernel, shape((size, args[0].shape[1]), args[0].dtype), *args)

    their_tokens = swap(tokens)
    half, share, basis, mine, own_tokens = call(
        start_kernel,
        (
            shape((rows, features), BF16),
            shape((part, features), BF16),
            shape((features, features), F32),
            shape((features, count), BF16),
            shape((count, chips * rows), BF16),
        ),
        [HBM] * 5,
        12 * features * features * count,
        2 * count * width,
        [
            pltpu.SMEM((BLOCK,), jnp.int32),
            pltpu.VMEM((BLOCK, features), F32),
            pltpu.VMEM((rows, features), F32),
            pltpu.VMEM((count, features), BF16),
            pltpu.VMEM((BLOCK, features), F32),
            pltpu.SemaphoreType.DMA((4 + chips,)),
        ],
    )(*map(in_hbm, (column_order, jnp.asarray(dct_rows(features)), weight, cotangent, tokens)))
    theirs = swap(mine)
    shares = [over_chips(share, d) for d in range(1, chips)]

    code, rest = shape((sent, rows), BF16), shape((features - sent, rows), BF16)
    code_f32, rest_f32 = shape(code.shape, F32), shape(rest.shape, F32)
    codes, keep_code, own_code, far, near, keep, own_rest = call(
        partial_kernel,
        (shape((2 * sent, rows), BF16), code_f32, code_f32, rest, rest, rest_f32, rest_f32),
        vmem(4),
        2 * CORES * count * rows * chips * features,
        CORES * count * rows * chips * 2,
    )(mine, theirs, own_tokens, their_tokens)

    codes = over_chips(codes, 1)
    far = over_chips(far, 1)
    near = over_chips(near, 1)
    late_code = over_chips(simple(code_kernel, code, keep_code, codes), 2)
    late = over_chips(simple(relay_kernel, rest, keep, far), 2)

    kept, coded = call(
        old_kernel,
        (shape((rows, features), F32), shape((sent, rows), F32)),
        vmem(2),
        24 * rows * features * sent,
        rows * features * 8,
    )(basis, momentum)
    scale = float(count * members) ** (-0.5)
    packed = simple(functools.partial(pack_kernel, scale), code, coded, own_code, codes, late_code)
    paired = simple(add_kernel, code, packed, over_rep(packed, 1))
    new_momentum, update, new_weight = call(
        functools.partial(final_kernel, scale, replicas),
        (shape(momentum.shape, F32), shape(weight.shape, F32), shape(weight.shape, F32)),
        vmem(8),
        2 * rows * features * features,
        rows * features * 28,
        [pltpu.VMEM((3, rows, features), F32), pltpu.SemaphoreType.DMA((3,))],
        HBM,
    )(basis, kept, own_rest, near, late, weight, paired, over_rep(paired, 2))

    joined = join(*shares)
    spread = [over_rep(joined, e) for e in range(1, replicas)]
    front, gathered = join(half, joined), join(*spread)
    out = (shape((count, width), BF16),)
    kernel = functools.partial(early_kernel, replicas, rows)
    copies = CORES * (1 + len(ARRIVAL))
    scratch = [
        pltpu.VMEM((count, CORES * front.shape[0]), BF16),
        pltpu.SemaphoreType.DMA((copies,)),
    ]
    (part_grad,) = call(
        kernel, out, vmem(3), count * width * features, count * width, scratch, HBM
    )(cotangent, front, swap(front))
    kernel = functools.partial(later_kernel, replicas, rows)
    copies = CORES * (replicas - 1) * len(ARRIVAL)
    scratch = [
        pltpu.VMEM((count, CORES * gathered.shape[0]), BF16),
        pltpu.SemaphoreType.DMA((copies,)),
    ]
    specs = [HBM] + vmem(3)
    (input_grad,) = call(
        kernel, out, specs, count * width * features, count * width, scratch, HBM, {0: 0}
    )(part_grad, cotangent, gathered, swap(gathered))
    return input_grad, new_momentum, update, new_weight


def general(tokens, cotangent, weight, momentum, column_order):
    members, replicas = lax.axis_size("fsdp"), lax.axis_size("rep")
    features = weight.shape[1]
    whole = lax.all_gather(weight.astype(BF16), "fsdp", axis=0, tiled=True)
    input_grad = dot(cotangent, whole, ((1,), (1,))).astype(BF16)
    grad = lax.psum_scatter(
        dot(tokens, cotangent, ((0,), (0,))), "fsdp", scatter_dimension=0, tiled=True
    )
    moment = MOMENTUM_DECAY * momentum[0] + grad * float(tokens.shape[0] * members) ** (-0.5)
    lane_block = jnp.arange(features) // BLOCK
    chosen = jnp.asarray(dct_rows(features))[column_order[:SEL]]
    basis = jnp.concatenate(
        [jnp.where(lane_block == b, chosen, 0.0) for b in range(features // BLOCK)]
    )
    coded = dot(moment, basis, ((1,), (1,)), HIGHEST)
    new_momentum = (moment - dot(coded, basis, ((1,), (0,)), HIGHEST))[None]
    summed = jnp.sum(lax.all_gather(coded, "rep", axis=0), axis=0)
    update = dot(summed, basis, ((1,), (0,)), HIGHEST) / replicas
    return input_grad, new_momentum, update, weight - LEARN_RATE * update


def solution(mesh):
    in_specs = (
        P(("rep", "fsdp"), None),
        P(("rep", "fsdp"), None),
        P("fsdp", None),
        P("rep", "fsdp", None),
        P(),
    )
    out_specs = (P(("rep", "fsdp"), None), P("rep", "fsdp", None), P("fsdp", None), P("fsdp", None))
    members, replicas = mesh.shape["fsdp"], mesh.shape["rep"]
    line = members == CHIPS * CORES and replicas == CHIPS

    def on_device(*args):
        if not line:
            return general(*args)
        return tuned(*args)

    return jax.shard_map(
        on_device, mesh=mesh, in_specs=in_specs, out_specs=out_specs, check_vma=False
    )
```

```python
import functools
import math

import jax
import jax.numpy as jnp
import numpy as np
from jax import lax
from jax.experimental import pallas as pl
from jax.experimental.pallas import tpu as pltpu
from jax.sharding import PartitionSpec as P


BLOCK = 64
SEL = 16
CORES = 2
CHIPS = 4
ARRIVAL = (1, 2, 3)

MOMENTUM_DECAY = 0.9
LEARN_RATE = 0.05
HIGHEST = lax.Precision.HIGHEST
BF16, F32 = jnp.bfloat16, jnp.float32


HBM = pl.BlockSpec(memory_space=pltpu.HBM)


def vmem(count):
    return [pl.BlockSpec(memory_space=pltpu.VMEM)] * count


def dct_rows(width):
    index = np.arange(BLOCK, dtype=np.float64)
    table = np.cos(math.pi * (2.0 * index[None, :] + 1.0) * index[:, None] / (2.0 * BLOCK))
    table *= math.sqrt(2.0 / BLOCK)
    table[0] *= math.sqrt(0.5)
    return np.tile(table, (1, width // BLOCK)).astype(np.float32)


def call(kernel, outs, in_specs, flops, nbytes, scratch=(), out_spec=None, aliases=None):
    run = pl.pallas_call(
        kernel,
        out_shape=outs,
        in_specs=in_specs,
        out_specs=[out_spec or pl.BlockSpec(memory_space=pltpu.VMEM)] * len(outs),
        input_output_aliases=aliases or {},
        scratch_shapes=scratch,
        cost_estimate=pl.CostEstimate(flops=flops, bytes_accessed=nbytes, transcendentals=0),
        compiler_params=pltpu.CompilerParams(vmem_limit_bytes=32 << 20),
    )
    return run


def dot(a, b, dims, precision=None):
    return lax.dot_general(
        a, b, (dims, ((), ())), precision=precision, preferred_element_type=F32
    )


def halves(x):
    high = x.astype(BF16)
    return high, (x - high.astype(F32)).astype(BF16)


def outer(a, b):
    (a_high, a_low), (b_high, b_low) = halves(a), halves(b)
    left = jnp.concatenate([a_high, a_low, a_high])
    return dot(left, jnp.concatenate([b_high, b_high, b_low]), ((0,), (0,)))


def position():
    member = lax.axis_index("fsdp")
    return lax.axis_index("rep"), member // CORES, lax.rem(member, CORES)


def in_hbm(x):
    return pltpu.with_memory_space_constraint(x, pltpu.HBM)


def wide(ref):
    return ref[...].astype(F32)


def start_kernel(order, rows, weight, cot, tokens, *refs):
    half, share, basis, coded_cot, own = refs[:5]
    held_order, held_rows, held_weight, held_cot, table, sems = refs[5:]
    rep, _, core = position()
    columns = weight.shape[0]
    moves = [(weight, held_weight), (order, held_order), (rows, held_rows), (cot, held_cot)]
    for k in range(own.shape[1] // columns):
        at = pl.ds(pl.multiple_of((CORES * k + core) * columns, columns), columns)
        moves.append((tokens.at[:, at], own.at[:, pl.ds(k * columns, columns)]))
    copies = [pltpu.make_async_copy(a, b, sems.at[k]) for k, (a, b) in enumerate(moves)]
    for copy in copies:
        copy.start()
    copies[0].wait()
    half[...] = held_weight[...].astype(BF16)
    part = share.shape[0]
    begin = pl.multiple_of(rep * part, part)
    share[...] = held_weight[pl.ds(begin, part), :].astype(BF16)
    copies[1].wait()
    copies[2].wait()
    for s in range(BLOCK):
        table[pl.ds(s, 1), :] = held_rows[pl.ds(held_order[s], 1), :]
    features = basis.shape[1]
    blocks = features // BLOCK
    rest = BLOCK - SEL
    for b in range(blocks):
        inside = lax.broadcasted_iota(jnp.int32, (BLOCK, features), 1) // BLOCK == b
        block = jnp.where(inside, table[...], 0.0)
        basis[pl.ds(b * SEL, SEL), :] = block[:SEL]
        basis[pl.ds(blocks * SEL + b * rest, rest), :] = block[SEL:]
    copies[3].wait()
    high, low = halves(basis[...])
    value = dot(high, held_cot[...], ((1,), (1,))) + dot(low, held_cot[...], ((1,), (1,)))
    coded_cot[...] = value.astype(BF16)
    for copy in copies[4:]:
        copy.wait()


def partial_kernel(mine, theirs, own_tok, their_tok, *outs):
    code, keep_code, own_code, far, near, keep, own_rest = outs
    _, chip, core = position()
    sent, columns = own_code.shape

    def total(mask):
        dest = chip ^ mask
        own_at = pl.ds(pl.multiple_of(dest * columns, columns), columns)
        at = pl.ds(pl.multiple_of((CORES * dest + core) * columns, columns), columns)
        value = dot(mine[...], own_tok[:, own_at], ((1,), (0,)))
        return value + dot(theirs[...], their_tok[:, at], ((1,), (0,)))

    first, last = code.at[pl.ds(0, sent), :], code.at[pl.ds(sent, sent), :]
    for mask, head, rest in (
        (1, first, near),
        (3, last, far),
        (2, keep_code, keep),
        (0, own_code, own_rest),
    ):
        value = total(mask)
        head[...] = value[:sent].astype(head.dtype)
        rest[...] = value[sent:].astype(rest.dtype)


def old_kernel(basis, momentum, kept, coded):
    sent = basis[: coded.shape[0], :]
    old = MOMENTUM_DECAY * momentum[0]
    (sent_high, sent_low), (high, low) = halves(sent), halves(old)
    code = dot(sent_high, high, ((1,), (1,))) + dot(sent_high, low, ((1,), (1,)))
    code += dot(sent_low, high, ((1,), (1,)))
    coded[...] = code
    kept[...] = old - outer(code, sent)


def join_kernel(*refs):
    at = 0
    for ref in refs[:-1]:
        refs[-1][pl.ds(at, ref.shape[0]), :] = ref[...]
        at += ref.shape[0]


def relay_kernel(keep, arrived, out):
    out[...] = (keep[...] + wide(arrived)).astype(out.dtype)


def code_kernel(keep, arrived, out):
    out[...] = (keep[...] + arrived[keep.shape[0] :, :].astype(F32)).astype(out.dtype)


def pack_kernel(scale, coded, own, arrived, late, out):
    total = own[...] + arrived[: own.shape[0], :].astype(F32) + wide(late)
    out[...] = (coded[...] + scale * total).astype(out.dtype)


def final_kernel(scale, replicas, basis, kept, own, near, late, weight, *refs):
    codes, (moment, update, new_weight, stage, sems) = refs[:-5], refs[-5:]
    total = own[...] + wide(near) + wide(late)
    rest = basis[basis.shape[0] - own.shape[0] :, :]
    grad = dot(total.astype(BF16), rest.astype(BF16), ((0,), (0,)))
    stage[0] = kept[...] + scale * grad
    copies = [
        pltpu.make_async_copy(stage.at[0], moment.at[0], sems.at[0]),
        pltpu.make_async_copy(stage.at[1], update, sems.at[1]),
        pltpu.make_async_copy(stage.at[2], new_weight, sems.at[2]),
    ]
    copies[0].start()
    pairs = [wide(a) + wide(b) for a, b in zip(codes[::2], codes[1::2])]
    code = sum(pairs[1:], pairs[0])
    value = outer(code, basis[: code.shape[0], :]) * (1.0 / replicas)
    stage[1] = value
    copies[1].start()
    stage[2] = weight[...] - LEARN_RATE * value
    copies[2].start()
    for copy in copies:
        copy.wait()


def send_blocks(cot, piece, blocks, stage, out, sems, done):
    start = sum(size for _, size in done)
    stage[:, pl.ds(start, piece.shape[0])] = dot(cot[...], piece, ((1,), (1,))).astype(stage.dtype)
    for begin, size in blocks:
        to = out.at[:, pl.ds(pl.multiple_of(begin, size), size)]
        copy = pltpu.make_async_copy(stage.at[:, pl.ds(start, size)], to, sems.at[len(done)])
        copy.start()
        done.append((copy, size))
        start += size


def places(rows, replicas, side, e):
    rep, chip, core = position()
    part = rows // replicas
    whose = lax.rem(core + side, CORES)
    return [((CORES * (chip ^ d) + whose) * rows + (rep ^ e) * part, part) for d in ARRIVAL]


def early_kernel(replicas, rows, cot, mine, theirs, out, stage, sems):
    _, chip, core = position()
    done = []
    for side, piece in enumerate((mine, theirs)):
        begin = (CORES * chip + lax.rem(core + side, CORES)) * rows
        blocks = places(rows, replicas, side, 0)
        send_blocks(cot, piece[:rows, :], [(begin, rows)], stage, out, sems, done)
        send_blocks(cot, piece[rows:, :], blocks, stage, out, sems, done)
    for copy, _ in done:
        copy.wait()


def later_kernel(replicas, rows, _, cot, mine, theirs, out, stage, sems):
    done = []
    group = rows // replicas * len(ARRIVAL)
    for side, piece in enumerate((mine, theirs)):
        for e in range(1, replicas):
            block = piece[(e - 1) * group : e * group, :]
            send_blocks(cot, block, places(rows, replicas, side, e), stage, out, sems, done)
    for copy, _ in done:
        copy.wait()


def tuned(tokens, cotangent, weight, momentum, column_order):
    members, replicas = lax.axis_size("fsdp"), lax.axis_size("rep")
    chips = members // CORES
    count, width = tokens.shape
    rows, features = weight.shape
    sent = features // BLOCK * SEL
    part = rows // replicas
    shape = jax.ShapeDtypeStruct

    def permute(x, axis, target):
        pairs = [(i, target(i)) for i in range(lax.axis_size(axis))]
        return lax.ppermute(x, axis, pairs)

    def swap(x):
        return permute(x, "fsdp", lambda i: i ^ 1)

    def over_chips(x, mask):
        return permute(x, "fsdp", lambda i: i ^ (CORES * mask))

    def over_rep(x, mask):
        return permute(x, "rep", lambda i: i ^ mask)

    def simple(kernel, out, *args):
        (value,) = call(kernel, (out,), vmem(len(args)), 0, 8 * out.size)(*args)
        return value

    def join(*args):
        size = sum(x.shape[0] for x in args)
        return simple(join_kernel, shape((size, args[0].shape[1]), args[0].dtype), *args)

    their_tokens = swap(tokens)
    half, share, basis, mine, own_tokens = call(
        start_kernel,
        (
            shape((rows, features), BF16),
            shape((part, features), BF16),
            shape((features, features), F32),
            shape((features, count), BF16),
            shape((count, chips * rows), BF16),
        ),
        [HBM] * 5,
        12 * features * features * count,
        2 * count * width,
        [
            pltpu.SMEM((BLOCK,), jnp.int32),
            pltpu.VMEM((BLOCK, features), F32),
            pltpu.VMEM((rows, features), F32),
            pltpu.VMEM((count, features), BF16),
            pltpu.VMEM((BLOCK, features), F32),
            pltpu.SemaphoreType.DMA((4 + chips,)),
        ],
    )(*map(in_hbm, (column_order, jnp.asarray(dct_rows(features)), weight, cotangent, tokens)))
    theirs = swap(mine)
    shares = [over_chips(share, d) for d in range(1, chips)]

    code, rest = shape((sent, rows), BF16), shape((features - sent, rows), BF16)
    code_f32, rest_f32 = shape(code.shape, F32), shape(rest.shape, F32)
    codes, keep_code, own_code, far, near, keep, own_rest = call(
        partial_kernel,
        (shape((2 * sent, rows), BF16), code_f32, code_f32, rest, rest, rest_f32, rest_f32),
        vmem(4),
        2 * CORES * count * rows * chips * features,
        CORES * count * rows * chips * 2,
    )(mine, theirs, own_tokens, their_tokens)

    codes = over_chips(codes, 1)
    far = over_chips(far, 1)
    near = over_chips(near, 1)
    late_code = over_chips(simple(code_kernel, code, keep_code, codes), 2)
    late = over_chips(simple(relay_kernel, rest, keep, far), 2)

    kept, coded = call(
        old_kernel,
        (shape((rows, features), F32), shape((sent, rows), F32)),
        vmem(2),
        24 * rows * features * sent,
        rows * features * 8,
    )(basis, momentum)
    scale = float(count * members) ** (-0.5)
    packed = simple(functools.partial(pack_kernel, scale), code, coded, own_code, codes, late_code)
    codes = [packed] + [over_rep(packed, e) for e in range(1, replicas)]
    new_momentum, update, new_weight = call(
        functools.partial(final_kernel, scale, replicas),
        (shape(momentum.shape, F32), shape(weight.shape, F32), shape(weight.shape, F32)),
        vmem(6 + replicas),
        2 * rows * features * features,
        rows * features * 28,
        [pltpu.VMEM((3, rows, features), F32), pltpu.SemaphoreType.DMA((3,))],
        HBM,
    )(basis, kept, own_rest, near, late, weight, *codes)

    joined = join(*shares)
    spread = [over_rep(joined, e) for e in range(1, replicas)]
    front, gathered = join(half, joined), join(*spread)
    out = (shape((count, width), BF16),)
    kernel = functools.partial(early_kernel, replicas, rows)
    copies = CORES * (1 + len(ARRIVAL))
    scratch = [
        pltpu.VMEM((count, CORES * front.shape[0]), BF16),
        pltpu.SemaphoreType.DMA((copies,)),
    ]
    (part_grad,) = call(
        kernel, out, vmem(3), count * width * features, count * width, scratch, HBM
    )(cotangent, front, swap(front))
    kernel = functools.partial(later_kernel, replicas, rows)
    copies = CORES * (replicas - 1) * len(ARRIVAL)
    scratch = [
        pltpu.VMEM((count, CORES * gathered.shape[0]), BF16),
        pltpu.SemaphoreType.DMA((copies,)),
    ]
    specs = [HBM] + vmem(3)
    (input_grad,) = call(
        kernel, out, specs, count * width * features, count * width, scratch, HBM, {0: 0}
    )(part_grad, cotangent, gathered, swap(gathered))
    return input_grad, new_momentum, update, new_weight


def general(tokens, cotangent, weight, momentum, column_order):
    members, replicas = lax.axis_size("fsdp"), lax.axis_size("rep")
    features = weight.shape[1]
    whole = lax.all_gather(weight.astype(BF16), "fsdp", axis=0, tiled=True)
    input_grad = dot(cotangent, whole, ((1,), (1,))).astype(BF16)
    grad = lax.psum_scatter(
        dot(tokens, cotangent, ((0,), (0,))), "fsdp", scatter_dimension=0, tiled=True
    )
    moment = MOMENTUM_DECAY * momentum[0] + grad * float(tokens.shape[0] * members) ** (-0.5)
    lane_block = jnp.arange(features) // BLOCK
    chosen = jnp.asarray(dct_rows(features))[column_order[:SEL]]
    basis = jnp.concatenate(
        [jnp.where(lane_block == b, chosen, 0.0) for b in range(features // BLOCK)]
    )
    coded = dot(moment, basis, ((1,), (1,)), HIGHEST)
    new_momentum = (moment - dot(coded, basis, ((1,), (0,)), HIGHEST))[None]
    summed = jnp.sum(lax.all_gather(coded, "rep", axis=0), axis=0)
    update = dot(summed, basis, ((1,), (0,)), HIGHEST) / replicas
    return input_grad, new_momentum, update, weight - LEARN_RATE * update


def solution(mesh):
    in_specs = (
        P(("rep", "fsdp"), None),
        P(("rep", "fsdp"), None),
        P("fsdp", None),
        P("rep", "fsdp", None),
        P(),
    )
    out_specs = (P(("rep", "fsdp"), None), P("rep", "fsdp", None), P("fsdp", None), P("fsdp", None))
    members, replicas = mesh.shape["fsdp"], mesh.shape["rep"]
    line = members == CHIPS * CORES and replicas == CHIPS

    def on_device(*args):
        if not line:
            return general(*args)
        return tuned(*args)

    return jax.shard_map(
        on_device, mesh=mesh, in_specs=in_specs, out_specs=out_specs, check_vma=False
    )
```
